32 devices in a mesh: groups: 2 (over x), dp: 16 (over z, y, core).
Axes of the slice: x: 2, y: 2, z: 4, core: 2. Of those that a mesh axis runs over, the one named last changes fastest.
Arguments:
- wave: float32 [2048, 320], P(('groups', 'dp')), parts along dimension 0, may hold values from -7.5 to 7.5
- row_slot: int32 [2048], P(('groups', 'dp')), parts along dimension 0, may hold values from 0 to 1023, as said below
- frame_lengths: int32 [128], P('groups'), parts along dimension 0, may hold values from 1 to 256, 1024 in all
- sample_trim: int32 [128], P('groups'), parts along dimension 0, may hold values from 0 to 319
- first_weight: float32 [10, 512], replicated, may hold values from -2 to 2
- mid_weight: bfloat16 [4, 3, 512, 512], replicated, may hold values from -0.15625 to 0.15625
- tail_weight: bfloat16 [2, 2, 512, 512], replicated, may hold values from -0.1875 to 0.1875
Outputs:
- centered: bfloat16 [2048, 512], P(('groups', 'dp')), parts along dimension 0
The draws below stay inside these ranges and needn't reach their ends.
There are 2 independent parts, one for each index of `groups`. The reference program is written for one: setup_inputs(seed, part) draws one part's arguments, and reference() takes and returns one part's arrays. A program takes and returns all parts, laid end to end along the dimension named above; an argument that names none is the same for every part. Nothing has to cross between parts.
Inputs may be any that keep to these rules, and one draw needn't show every extreme that they name: row_slot is a permutation of 0 .. 1023. For every index h of dp and every index o, at most 6 of the 64 rows of h have row_slot in [o * 64, (o + 1) * 64), and for every h exactly one o receives 6 of them. frame_lengths sum to 1024, and the largest is 256.
All inputs are finite; a program needn't handle non-finite values.
Results may differ from the reference program's by a relative error of at most 0.023.
Values sent between devices are 32-bit elements; how exact they have to be, the bound alone decides.
A program may use at most 64 MiB of HBM per device.

```python
import math
import jax
import jax.numpy as jnp
import numpy as np
from jax import lax

C1 = 512
BLOCK = 320
LOOK = 80
MID = 4
TAIL = 2
F_DEV = 64
FRAMES = 1024
ROLLS = 64
MAXLEN = 256
CAP = 6


def make_slots(key):
    owners = FRAMES // F_DEV
    keys_all = jax.random.split(jax.random.fold_in(key, 11), 5)
    ranking = jax.random.permutation(keys_all[0], owners)
    leftover_rows = F_DEV - CAP
    baseline = leftover_rows // (owners - 1)
    leftover = leftover_rows % (owners - 1)
    position = jnp.arange(owners, dtype=jnp.int32)
    sorted_load = jnp.where(position == 0, CAP, baseline + (position - 1 < leftover).astype(jnp.int32))
    multiplicity = jnp.zeros((owners,), jnp.int32).at[ranking].set(sorted_load)
    owner_perm = jax.random.permutation(keys_all[1], owners)
    holder_perm = jax.random.permutation(keys_all[2], owners)
    counts = multiplicity[(owner_perm[None, :] - holder_perm[:, None]) % owners]
    cumulative = jnp.cumsum(counts, axis=0)
    within = jnp.arange(F_DEV, dtype=jnp.int32)
    sources = jnp.sum((cumulative.T[:, None, :] <= within[None, :, None]).astype(jnp.int32), axis=2)
    shuffles = jax.vmap(lambda single_key: jax.random.permutation(single_key, F_DEV))(jax.random.split(keys_all[3], owners))
    shuffled = jnp.take_along_axis(sources, shuffles, axis=1).reshape(-1)
    scores = shuffled * FRAMES + jax.random.permutation(keys_all[4], FRAMES)
    return jnp.argsort(scores, stable=True).astype(jnp.int32)


def draw_row_slot(key, part):
    return make_slots(key)


def draw_wave(key, part):
    slots = make_slots(key)
    region_frames = F_DEV // 2
    regions = FRAMES // region_frames
    keys_all = jax.random.split(jax.random.fold_in(key, 23), 6)
    offset = jax.random.uniform(keys_all[0], (regions,), jnp.float32, -1.5, 1.5)
    strength = jax.random.uniform(keys_all[1], (regions,), jnp.float32, 0.0, 1.5)
    omega = jnp.exp(jax.random.uniform(keys_all[2], (regions,), jnp.float32, math.log(0.02), math.log(0.6)))
    phase = jax.random.uniform(keys_all[3], (regions,), jnp.float32, -math.pi, math.pi)
    loudness = jnp.exp(jax.random.uniform(keys_all[4], (regions,), jnp.float32, math.log(0.25), math.log(1.5)))
    noise = jnp.clip(jax.random.normal(keys_all[5], (FRAMES, BLOCK), jnp.float32), -3.0, 3.0)
    region_of = slots // region_frames
    sample_pos = jnp.arange(BLOCK, dtype=jnp.float32)[None, :]
    tone = strength[region_of][:, None] * jnp.sin(omega[region_of][:, None] * sample_pos + phase[region_of][:, None])
    return offset[region_of][:, None] + loudness[region_of][:, None] * noise + tone


def with_ends(entries, key, smallest, top_value):
    dims = entries.shape
    place = [jax.random.randint(jax.random.fold_in(key, axis), (), 0, dims[axis]) for axis in range(len(dims))]
    entries = entries.at[tuple(place)].set(smallest)
    longest = dims.index(max(dims))
    place[longest] = (place[longest] + 1) % dims[longest]
    return entries.at[tuple(place)].set(top_value)


def length_profile(count, total, reach, skew):
    portions = [(1 << 20) // math.isqrt(standing ** skew) + 1 for standing in range(2, count + 1)]
    spare, given = total - reach - (count - 1), [1] * (count - 1)
    while spare > 0:
        movable = [i for i in range(count - 1) if given[i] < reach]
        mass, left = sum([portions[i] for i in movable]), spare
        for i in movable:
            addition = min(reach - given[i], max(1, left * portions[i] // mass), spare)
            given[i] = given[i] + addition
            spare = spare - addition
    return np.array([reach] + given)


def ragged_sizes(rng, count, total, reach, skew):
    if count == 2:
        one = jax.random.randint(rng, (), max(1, total - reach), min(reach, total - 1) + 1)
        return jnp.stack([one, total - one])
    lengths = jnp.asarray(length_profile(count, total, reach, skew), jnp.int32)
    pairs = (count - 1) // 2
    donor, receiver = lengths[1:1 + 2 * pairs:2], lengths[2:2 + 2 * pairs:2]
    margin = jnp.minimum(donor - 1, reach - receiver)
    moved = jax.random.randint(jax.random.fold_in(rng, 1), (pairs,), 0, 1 << 20) % (margin + 1)
    lengths = lengths.at[1:1 + 2 * pairs:2].set(donor - moved).at[2:2 + 2 * pairs:2].set(receiver + moved)
    return lengths[jax.random.permutation(jax.random.fold_in(rng, 2), count)]


def scatter_about(own_key, dims, width, most, kind=jnp.bfloat16):
    array = width * jax.random.normal(own_key, dims, jnp.float32)
    return jnp.clip(array, min=-most, max=most).astype(kind)


def setup_inputs(seed: int = 0, part: int = 0) -> dict:
    splits = jax.random.split(jax.random.key(seed), 8)
    part_splits = jax.random.split(jax.random.fold_in(splits[7], part), 8)
    wave = draw_wave(jax.random.fold_in(jax.random.fold_in(splits[7], part), 71), part)
    row_slot = draw_row_slot(jax.random.fold_in(jax.random.fold_in(splits[7], part), 71), part)
    frame_lengths = ragged_sizes(part_splits[2], ROLLS, FRAMES, MAXLEN, 2).astype(jnp.int32)
    sample_trim = with_ends(jax.random.randint(part_splits[3], (ROLLS,), 0, BLOCK), jax.random.fold_in(part_splits[3], 1), 0, BLOCK - 1).astype(jnp.int32)
    first_weight = scatter_about(splits[4], (10, C1), 10 ** -0.5, 2.0, jnp.float32)
    mid_weight = scatter_about(splits[5], (MID, 3, C1, C1), (3 * C1) ** -0.5, 0.15625)
    tail_weight = scatter_about(splits[6], (TAIL, 2, C1, C1), (2 * C1) ** -0.5, 0.1875)
    return {"wave": wave, "row_slot": row_slot, "frame_lengths": frame_lengths, "sample_trim": sample_trim, "first_weight": first_weight, "mid_weight": mid_weight, "tail_weight": tail_weight}


def norm_gelu(values):
    average = lax.optimization_barrier(jnp.mean(values, axis=-1, keepdims=True))
    centred = values - average
    spread = lax.optimization_barrier(jnp.mean(centred * centred, axis=-1, keepdims=True))
    return jax.nn.gelu(centred / jnp.sqrt(spread + 1e-05), approximate=False).astype(jnp.bfloat16)

def strided(inputs, weight, stride):
    kernel = weight.shape[0]
    length = (inputs.shape[0] - kernel) // stride + 1
    summed = jnp.zeros((length, weight.shape[2]), jnp.float32)
    for offset in range(kernel):
        shifted = lax.slice_in_dim(inputs, offset, offset + stride * (length - 1) + 1, stride, 0)
        summed = summed + jnp.dot(shifted, weight[offset], preferred_element_type=jnp.float32)
    return summed

def frontend(samples, first_weight, mid_weight, tail_weight):
    fifths = samples.reshape(-1, 5)
    patches = jnp.concatenate([fifths[:-1], fifths[1:]], axis=1)
    hidden = norm_gelu(jnp.dot(patches, first_weight, precision=lax.Precision.HIGHEST, preferred_element_type=jnp.float32))
    for step_index in range(MID):
        hidden = norm_gelu(strided(hidden, mid_weight[step_index], 2))
    for step_index in range(TAIL):
        hidden = norm_gelu(strided(hidden, tail_weight[step_index], 2))
    return hidden

def reference(wave, row_slot, frame_lengths, sample_trim, first_weight, mid_weight, tail_weight):
    stream = jnp.zeros((FRAMES, BLOCK), jnp.float32).at[row_slot].set(wave)
    starts = jnp.cumsum(frame_lengths) - frame_lengths
    frame_ids = jnp.arange(FRAMES, dtype=jnp.int32)
    rollout = lax.optimization_barrier(jnp.sum((starts[None, :] <= frame_ids[:, None]).astype(jnp.int32), axis=1)) - 1
    sample_limit = BLOCK * frame_lengths - sample_trim
    within = ((frame_ids - starts[rollout]) * BLOCK)[:, None] + jnp.arange(BLOCK, dtype=jnp.int32)[None, :]
    signal = jnp.where(within < sample_limit[rollout][:, None], stream, 0.0)
    padded = jnp.concatenate([signal.reshape(-1), jnp.zeros((LOOK,), jnp.float32)])

    def one_block(block_index):
        begin = (block_index * (F_DEV * BLOCK)).astype(jnp.int32)
        samples = lax.dynamic_slice_in_dim(padded, begin, F_DEV * BLOCK + LOOK)
        return frontend(samples, first_weight, mid_weight, tail_weight)
    blocks = FRAMES // F_DEV
    features = lax.map(one_block, jnp.arange(blocks, dtype=jnp.int32)).reshape(FRAMES, -1)
    rollout_sum = jax.ops.segment_sum(features.astype(jnp.float32), rollout, num_segments=ROLLS)
    rollout_mean = rollout_sum / frame_lengths[:, None].astype(jnp.float32)
    return (features.astype(jnp.float32) - rollout_mean[rollout]).astype(jnp.bfloat16)
```

```python
import functools

import jax
import jax.numpy as jnp
from jax import lax
from jax.experimental import pallas as pl
from jax.experimental.pallas import tpu as pltpu
from jax.sharding import PartitionSpec as P

BLOCK = 320
WIDE = 384
MAXLEN = 256
EPS = 1e-05
HALF_ROOT = 0.7071067811865476
HIGHEST = lax.Precision.HIGHEST
F32 = jnp.float32
BF16 = jnp.bfloat16


def iota(shape, dim):
    return lax.broadcasted_iota(jnp.int32, shape, dim).astype(F32)


def to_column(row):
    size = row.shape[1]
    same = iota((size, size), 0) == iota((size, size), 1)
    return jnp.sum(jnp.where(same, row, 0.0), axis=1, keepdims=True)


def starts_column(length_row):
    size = length_row.shape[1]
    earlier = iota((size, size), 1) < iota((size, size), 0)
    return jnp.sum(jnp.where(earlier, length_row, 0.0), axis=1, keepdims=True)


def norm_gelu(values):
    average = jnp.mean(values, axis=-1, keepdims=True)
    centred = values - average
    spread = jnp.mean(centred * centred, axis=-1, keepdims=True)
    scaled = centred * (lax.rsqrt(spread + EPS) * HALF_ROOT)
    half = scaled * HALF_ROOT
    return half + half * lax.erf(scaled)


def route_kernel(n, cap, stride, wave_ref, slot_ref, out_ref, wide, send, recv, send_sem, recv_sem):
    me = lax.axis_index("dp")

    def greet(k, carry):
        pl.semaphore_signal(
            pltpu.get_barrier_semaphore(), inc=1, device_id={"dp": lax.rem(me + k, n)}
        )
        return carry

    lax.fori_loop(1, n, greet, 0)
    rows = wave_ref.shape[0]
    slot_row = slot_ref[...].astype(F32)
    slot_col = to_column(slot_row)
    target_row = jnp.floor(slot_row / rows)
    target_col = jnp.floor(slot_col / rows)
    earlier = (iota((rows, rows), 0) < iota((rows, rows), 1)) & (target_col == target_row)
    rank_row = jnp.sum(jnp.where(earlier, 1.0, 0.0), axis=0, keepdims=True)
    dest_row = target_row * stride + rank_row
    ahead_row = jnp.where(target_row * rows == slot_row, (target_row - 1.0) * stride + cap, -1.0)
    place = iota((n * stride, rows), 0)
    pick = jnp.where((place == dest_row) | (place == ahead_row), 1.0, 0.0)
    wide[:, :BLOCK] = wave_ref[...]
    wide[:, BLOCK:] = jnp.where(iota((rows, WIDE - BLOCK), 1) == 0.0, slot_col + 1.0, 0.0)
    send[...] = jnp.dot(pick, wide[...], precision=HIGHEST, preferred_element_type=F32)
    mine = pl.ds(pl.multiple_of(me * stride, stride), stride)
    recv[mine, :] = send[mine, :]
    pl.semaphore_wait(pltpu.get_barrier_semaphore(), n - 1)

    def copy_to(k):
        to = lax.rem(me + k, n)
        return pltpu.make_async_remote_copy(
            src_ref=send.at[pl.ds(pl.multiple_of(to * stride, stride), stride)],
            dst_ref=recv.at[mine],
            send_sem=send_sem.at[to],
            recv_sem=recv_sem.at[me],
            device_id={"dp": to},
        )

    def copy_from(k):
        source = lax.rem(me + n - k, n)
        return pltpu.make_async_remote_copy(
            src_ref=send.at[mine],
            dst_ref=recv.at[pl.ds(pl.multiple_of(source * stride, stride), stride)],
            send_sem=send_sem.at[me],
            recv_sem=recv_sem.at[source],
            device_id={"dp": source},
        )

    def begin(k, carry):
        copy_to(k).start()
        return carry

    def finish(k, carry):
        copy_from(k).wait_recv()
        copy_to(k).wait_send()
        return carry

    lax.fori_loop(1, n, begin, 0)
    lax.fori_loop(1, n, finish, 0)
    out_ref[...] = recv[...]


def conv_kernel(
    recv_ref, length_ref, trim_ref, first_ref, mid_ref, tail_ref, out_ref,
    xs, e1, o1, e2, o2, e3, o3, e4, o4, e5, o5, e6, o6, h1, h2, h3, acc,
):
    me = lax.axis_index("dp").astype(F32)
    rows = out_ref.shape[0]
    length_row = length_ref[...].astype(F32)
    trim_col = to_column(trim_ref[...].astype(F32))
    start = starts_column(length_row)
    end = start + to_column(length_row)
    count = length_row.shape[1]
    frame = iota((count, 128), 1) + me * rows
    limit = jnp.sum(
        jnp.where((start <= frame) & (frame < end), BLOCK * (end - frame) - trim_col, 0.0),
        axis=0,
        keepdims=True,
    )
    got = recv_ref.shape[0]
    slot = recv_ref[:, BLOCK : BLOCK + 1] - 1.0 - me * rows
    lane = iota((got, 128), 1)
    spread = jnp.where((slot == lane) & (lane <= rows), 1.0, 0.0)
    wave = jnp.transpose(recv_ref[...])[:BLOCK]
    stream = jnp.dot(wave, spread, precision=HIGHEST, preferred_element_type=F32)
    signal = jnp.where(iota((BLOCK, 128), 0) < limit, stream, 0.0)
    part1 = signal.astype(BF16).astype(F32)
    rest = signal - part1
    part2 = rest.astype(BF16).astype(F32)
    part3 = rest - part2
    for index, part in enumerate((part1, part2, part3)):
        xs[index, :BLOCK, :] = part
        xs[index, BLOCK : BLOCK + 8, :] = pltpu.roll(part[:8], 127, 1)
        xs[index, BLOCK + 8 :, :] = jnp.zeros((8, 128), F32)

    first = first_ref[...]
    weight1 = first.astype(BF16).astype(F32)
    left = first - weight1
    weight2 = left.astype(BF16).astype(F32)
    weight3 = left - weight2
    kernel1 = jnp.concatenate([weight1, weight2, weight1, weight2, weight3, weight1], axis=0).astype(BF16)

    def patches(phase):
        a, b, c = [xs[index, pl.ds(5 * phase, 16), :] for index in range(3)]
        return jnp.concatenate([a, a, b, b, a, c], axis=0)

    def first_dot(block):
        return lax.dot_general(
            block.astype(BF16), kernel1, (((0,), (0,)), ((), ())), preferred_element_type=F32
        )

    def gather_halo(phase, total):
        return jnp.where(
            lax.broadcasted_iota(jnp.int32, (96, 128), 1) == phase, patches(phase)[:, rows : rows + 1], total
        )

    halo = lax.fori_loop(0, 16, gather_halo, jnp.zeros((96, 128), F32))
    h1[:16, :] = norm_gelu(first_dot(halo[:, :16])).astype(BF16).astype(F32)
    h1[16:, :] = jnp.zeros_like(h1[16:, :])

    def first_step(step, carry):
        where = pl.ds(pl.multiple_of(step * rows, rows), rows)
        for parity, dest in ((0, e1), (1, o1)):
            acc[parity * rows : (parity + 1) * rows, :] = first_dot(patches(2 * step + parity)[:, :rows])
        for parity, dest in ((0, e1), (1, o1)):
            for r in range(0, rows, 16):
                block = acc[parity * rows + r : parity * rows + r + 16, :]
                dest[pl.ds(pl.multiple_of(step * rows + r, 16), 16), :] = norm_gelu(block).astype(BF16)
        return carry

    lax.fori_loop(0, 32, first_step, 0)

    def wrap(even, halo_ref, phases):
        rolled = pltpu.roll(even[:rows, :].astype(F32), rows - 1, 0)
        shifted = jnp.where(iota(rolled.shape, 0) == rows - 1, halo_ref[0:1, :], rolled)
        even[pl.ds(phases // 2 * rows, rows), :] = shifted.astype(BF16)

    def layer(even, odd, taps, dest_even, dest_odd, phases):
        chunk = min(phases, 4)
        size = chunk * rows

        def step(index, carry):
            base = pl.multiple_of(index * size, size)
            inputs = [even[pl.ds(base, size), :], odd[pl.ds(base, size), :]]
            if len(taps) == 3:
                inputs.append(even[pl.ds(pl.multiple_of(base + rows, rows), size), :])
            total = None
            for value, tap in zip(inputs, taps):
                term = jnp.dot(value, tap[...], preferred_element_type=F32)
                total = term if total is None else total + term
            acc[:size, :] = total
            for p in range(chunk):
                dest = dest_even if p % 2 == 0 else dest_odd
                for r in range(0, rows, 16):
                    block = acc[p * rows + r : p * rows + r + 16, :]
                    at = index * (size // 2) + p // 2 * rows + r
                    if chunk == 1:
                        at = r
                    dest[pl.ds(pl.multiple_of(at, 16), 16), :] = norm_gelu(block).astype(BF16)
            return carry

        if phases == chunk:
            step(0, 0)
        else:
            lax.fori_loop(0, phases // chunk, step, 0)

    def halo_layer(source, dest, taps):
        total = None
        for offset, tap in enumerate(taps):
            choose = jnp.where(iota((16, 24), 1) == 2.0 * iota((16, 24), 0) + offset, 1.0, 0.0)
            value = jnp.dot(
                choose.astype(BF16), source[...].astype(BF16), preferred_element_type=F32
            ).astype(BF16)
            term = jnp.dot(value, tap[...], preferred_element_type=F32)
            total = term if total is None else total + term
        dest[:8, :] = norm_gelu(total[:8]).astype(BF16).astype(F32)
        dest[8:, :] = jnp.zeros_like(dest[8:, :])

    mids = [[mid_ref.at[i, t] for t in range(3)] for i in range(4)]
    tails = [[tail_ref.at[i, t] for t in range(2)] for i in range(2)]
    wrap(e1, h1, 64)
    halo_layer(h1, h2, mids[0])
    layer(e1, o1, mids[0], e2, o2, 32)
    wrap(e2, h2, 32)
    halo_layer(h2, h3, mids[1])
    layer(e2, o2, mids[1], e3, o3, 16)
    wrap(e3, h3, 16)
    halo_layer(h3, h1, mids[2])
    layer(e3, o3, mids[2], e4, o4, 8)
    wrap(e4, h1, 8)
    layer(e4, o4, mids[3], e5, o5, 4)
    layer(e5, o5, tails[0], e6, o6, 2)
    layer(e6, o6, tails[1], out_ref, out_ref, 1)


def mean_kernel(n, reach, feature_ref, length_ref, out_ref, send, recv, send_sem, recv_sem):
    me = lax.axis_index("dp")
    rows, channels = feature_ref.shape
    pieces = channels // 128
    recv[...] = jnp.zeros_like(recv)
    barrier = pltpu.get_barrier_semaphore()
    links = [(k, k - 1) for k in range(1, reach + 1)] + [(-k, reach + k - 1) for k in range(1, reach + 1)]

    def inside(k):
        return (me + k < n) & (me + k >= 0)

    for k, _ in links:
        @pl.when(inside(k))
        def _():
            pl.semaphore_signal(barrier, inc=1, device_id={"dp": me + k})

    base = me.astype(F32) * rows
    length_row = length_ref[...].astype(F32)
    start = starts_column(length_row)
    end = start + to_column(length_row)
    frame = iota((length_row.shape[1], rows), 1) + base
    member = (start <= frame) & (frame < end)
    start_row = jnp.sum(jnp.where(member, start, 0.0), axis=0, keepdims=True)
    end_row = jnp.sum(jnp.where(member, end, 0.0), axis=0, keepdims=True)
    start_col = to_column(start_row)
    end_col = to_column(end_row)
    features = feature_ref[...]
    line = iota((16, rows), 1) + base
    last = line >= start_row[:, rows - 1 : rows]
    initial = line < end_row[:, 0:1]
    pick = jnp.where(iota((16, rows), 0) == 0.0, jnp.where(last, 1.0, 0.0), jnp.where(initial, 1.0, 0.0))
    edges = jnp.dot(pick.astype(BF16), features, preferred_element_type=F32)
    send[...] = jnp.zeros_like(send)
    for index in range(2):
        for piece in range(pieces):
            send[index, piece : piece + 1, :] = edges[index : index + 1, piece * 128 : piece * 128 + 128]

    def copy(k, slot):
        return pltpu.make_async_remote_copy(
            src_ref=send.at[0 if k > 0 else 1],
            dst_ref=recv.at[slot],
            send_sem=send_sem.at[slot],
            recv_sem=recv_sem.at[slot],
            device_id={"dp": me + k},
        )

    for place in range(n):
        if place < reach or place >= n - reach:
            @pl.when(me == place)
            def _():
                pl.semaphore_wait(barrier, min(place, reach) + min(n - 1 - place, reach))

    @pl.when((me >= reach) & (me < n - reach))
    def _():
        pl.semaphore_wait(barrier, 2 * reach)

    for k, slot in links:
        @pl.when(inside(k))
        def _():
            copy(k, slot).start()
    local = iota((rows, rows), 1) + base
    within = jnp.where((start_col <= local) & (local < end_col), 1.0, 0.0).astype(BF16)
    totals = jnp.dot(within, features, preferred_element_type=F32)
    for k, slot in links:
        @pl.when(inside(-k))
        def _():
            copy(-k, slot).wait_recv()

        @pl.when(inside(k))
        def _():
            copy(k, slot).wait_send()
    for k, slot in links:
        row = jnp.concatenate([recv[slot, piece : piece + 1, :] for piece in range(pieces)], axis=1)
        if k > 0:
            reached = start_col <= base - (k - 1) * rows - 1.0
        else:
            reached = end_col > base - k * rows
        totals = totals + jnp.where(reached, row, 0.0)
    out_ref[...] = (features.astype(F32) - totals / (end_col - start_col)).astype(BF16)


def per_device(wave, row_slot, frame_lengths, sample_trim, first_weight, mid_weight, tail_weight):
    rows = wave.shape[0]
    channels = first_weight.shape[1]
    n = lax.axis_size("dp")
    cap = rows // n + 2
    stride = (cap + 1 + 7) // 8 * 8
    reach = min((MAXLEN + rows - 2) // rows, n - 1)
    vmem = pl.BlockSpec(memory_space=pltpu.VMEM)
    lengths = frame_lengths.reshape(1, -1)
    received = pl.pallas_call(
        functools.partial(route_kernel, n, cap, stride),
        out_shape=jax.ShapeDtypeStruct((n * stride, WIDE), F32),
        in_specs=[vmem] * 2,
        out_specs=vmem,
        scratch_shapes=[
            pltpu.VMEM((rows, WIDE), F32),
            pltpu.VMEM((n * stride, WIDE), F32),
            pltpu.VMEM((n * stride, WIDE), F32),
            pltpu.SemaphoreType.DMA((n,)),
            pltpu.SemaphoreType.DMA((n,)),
        ],
        compiler_params=pltpu.CompilerParams(collective_id=0, has_side_effects=True),
        name="route",
    )(wave, row_slot.reshape(1, -1))
    first = jnp.pad(first_weight, ((0, 6), (0, 0)))

    def slab(phases):
        return pltpu.VMEM((phases * rows, channels), BF16)

    features = pl.pallas_call(
        conv_kernel,
        out_shape=jax.ShapeDtypeStruct((rows, channels), BF16),
        in_specs=[vmem] * 6,
        out_specs=vmem,
        scratch_shapes=[
            pltpu.VMEM((3, BLOCK + 16, 128), F32),
            slab(33), slab(32), slab(17), slab(16), slab(9), slab(8), slab(5), slab(4),
            slab(2), slab(2), slab(1), slab(1),
            pltpu.VMEM((24, channels), F32),
            pltpu.VMEM((24, channels), F32),
            pltpu.VMEM((24, channels), F32),
            pltpu.VMEM((4 * rows, channels), F32),
        ],
        compiler_params=pltpu.CompilerParams(vmem_limit_bytes=48 * 1024 * 1024),
        name="convs",
    )(received, lengths, sample_trim.reshape(1, -1), first, mid_weight, tail_weight)
    return pl.pallas_call(
        functools.partial(mean_kernel, n, reach),
        out_shape=jax.ShapeDtypeStruct((rows, channels), BF16),
        in_specs=[vmem] * 2,
        out_specs=vmem,
        scratch_shapes=[
            pltpu.VMEM((2, 8, 128), F32),
            pltpu.VMEM((2 * reach, 8, 128), F32),
            pltpu.SemaphoreType.DMA((2 * reach,)),
            pltpu.SemaphoreType.DMA((2 * reach,)),
        ],
        compiler_params=pltpu.CompilerParams(collective_id=1, has_side_effects=True),
        name="means",
    )(features, lengths)


def solution(mesh):
    placed = (
        P(("groups", "dp"), None),
        P(("groups", "dp")),
        P("groups"),
        P("groups"),
        P(),
        P(),
        P(),
    )
    return jax.shard_map(
        per_device, mesh=mesh, in_specs=placed, out_specs=P(("groups", "dp"), None), check_vma=False
    )
```

```python
import functools

import jax
import jax.numpy as jnp
from jax import lax
from jax.experimental import pallas as pl
from jax.experimental.pallas import tpu as pltpu
from jax.sharding import PartitionSpec as P

BLOCK = 320
WIDE = 384
MAXLEN = 256
EPS = 1e-05
HALF_ROOT = 0.7071067811865476
HIGHEST = lax.Precision.HIGHEST
F32 = jnp.float32
BF16 = jnp.bfloat16


def iota(shape, dim):
    return lax.broadcasted_iota(jnp.int32, shape, dim).astype(F32)


def to_column(row):
    size = row.shape[1]
    same = iota((size, size), 0) == iota((size, size), 1)
    return jnp.sum(jnp.where(same, row, 0.0), axis=1, keepdims=True)


def starts_column(length_row):
    size = length_row.shape[1]
    earlier = iota((size, size), 1) < iota((size, size), 0)
    return jnp.sum(jnp.where(earlier, length_row, 0.0), axis=1, keepdims=True)


def norm_gelu(values):
    average = jnp.mean(values, axis=-1, keepdims=True)
    centred = values - average
    spread = jnp.mean(centred * centred, axis=-1, keepdims=True)
    scaled = centred * (lax.rsqrt(spread + EPS) * HALF_ROOT)
    half = scaled * HALF_ROOT
    return half + half * lax.erf(scaled)


def route(n, cap, stride, wave_ref, slot_ref, wide, send, recv, send_sem, recv_sem):
    me = lax.axis_index("dp")

    def greet(k, carry):
        pl.semaphore_signal(
            pltpu.get_barrier_semaphore(), inc=1, device_id={"dp": lax.rem(me + k, n)}
        )
        return carry

    lax.fori_loop(1, n, greet, 0)
    rows = wave_ref.shape[0]
    slot_row = slot_ref[...].astype(F32)
    slot_col = to_column(slot_row)
    target_row = jnp.floor(slot_row / rows)
    target_col = jnp.floor(slot_col / rows)
    earlier = (iota((rows, rows), 0) < iota((rows, rows), 1)) & (target_col == target_row)
    rank_row = jnp.sum(jnp.where(earlier, 1.0, 0.0), axis=0, keepdims=True)
    dest_row = target_row * stride + rank_row
    ahead_row = jnp.where(target_row * rows == slot_row, (target_row - 1.0) * stride + cap, -1.0)
    place = iota((n * stride, rows), 0)
    pick = jnp.where((place == dest_row) | (place == ahead_row), 1.0, 0.0)
    wide[:, :BLOCK] = wave_ref[...]
    wide[:, BLOCK:] = jnp.where(iota((rows, WIDE - BLOCK), 1) == 0.0, slot_col + 1.0, 0.0)
    send[...] = jnp.dot(pick, wide[...], precision=HIGHEST, preferred_element_type=F32)
    mine = pl.ds(pl.multiple_of(me * stride, stride), stride)
    recv[mine, :] = send[mine, :]
    pl.semaphore_wait(pltpu.get_barrier_semaphore(), n - 1)

    def copy_to(k):
        to = lax.rem(me + k, n)
        return pltpu.make_async_remote_copy(
            src_ref=send.at[pl.ds(pl.multiple_of(to * stride, stride), stride)],
            dst_ref=recv.at[mine],
            send_sem=send_sem.at[to],
            recv_sem=recv_sem.at[me],
            device_id={"dp": to},
        )

    def copy_from(k):
        source = lax.rem(me + n - k, n)
        return pltpu.make_async_remote_copy(
            src_ref=send.at[mine],
            dst_ref=recv.at[pl.ds(pl.multiple_of(source * stride, stride), stride)],
            send_sem=send_sem.at[me],
            recv_sem=recv_sem.at[source],
            device_id={"dp": source},
        )

    def begin(k, carry):
        copy_to(k).start()
        return carry

    def finish(k, carry):
        copy_from(k).wait_recv()
        copy_to(k).wait_send()
        return carry

    lax.fori_loop(1, n, begin, 0)
    lax.fori_loop(1, n, finish, 0)


def convs(
    ready, recv_ref, length_ref, trim_ref, first_ref, mid_ref, tail_ref, out_ref,
    xs, pad, e1, o1, e2, o2, e3, o3, e4, o4, e5, o5, e6, o6, h1, h2, h3, acc,
):
    me = lax.axis_index("dp").astype(F32)
    rows = out_ref.shape[0]
    length_row = length_ref[...].astype(F32)
    trim_col = to_column(trim_ref[...].astype(F32))
    start = starts_column(length_row)
    end = start + to_column(length_row)
    count = length_row.shape[1]
    frame = iota((count, 128), 1) + me * rows
    limit = jnp.sum(
        jnp.where((start <= frame) & (frame < end), BLOCK * (end - frame) - trim_col, 0.0),
        axis=0,
        keepdims=True,
    )
    got = recv_ref.shape[0]
    slot = recv_ref[:, BLOCK : BLOCK + 1] - 1.0 - me * rows
    lane = iota((got, 128), 1)
    spread = jnp.where((slot == lane) & (lane <= rows), 1.0, 0.0)
    wave = jnp.transpose(recv_ref[...])[:BLOCK]
    stream = jnp.dot(wave, spread, precision=HIGHEST, preferred_element_type=F32)
    signal = jnp.where(iota((BLOCK, 128), 0) < limit, stream, 0.0)
    part1 = signal.astype(BF16).astype(F32)
    rest = signal - part1
    part2 = rest.astype(BF16).astype(F32)
    part3 = rest - part2
    for index, part in enumerate((part1, part2, part3)):
        xs[index, :BLOCK, :] = part
        xs[index, BLOCK : BLOCK + 8, :] = pltpu.roll(part[:8], 127, 1)
        xs[index, BLOCK + 8 :, :] = jnp.zeros((8, 128), F32)

    pad[...] = jnp.zeros_like(pad)
    pad[: first_ref.shape[0], :] = first_ref[...]
    first = pad[...]
    weight1 = first.astype(BF16).astype(F32)
    left = first - weight1
    weight2 = left.astype(BF16).astype(F32)
    weight3 = left - weight2
    kernel1 = jnp.concatenate([weight1, weight2, weight1, weight2, weight3, weight1], axis=0).astype(BF16)

    def patches(phase):
        a, b, c = [xs[index, pl.ds(5 * phase, 16), :] for index in range(3)]
        return jnp.concatenate([a, a, b, b, a, c], axis=0)

    def first_dot(block):
        return lax.dot_general(
            block.astype(BF16), kernel1, (((0,), (0,)), ((), ())), preferred_element_type=F32
        )

    def gather_halo(phase, total):
        return jnp.where(
            lax.broadcasted_iota(jnp.int32, (96, 128), 1) == phase, patches(phase)[:, rows : rows + 1], total
        )

    halo = lax.fori_loop(0, 16, gather_halo, jnp.zeros((96, 128), F32))
    h1[:16, :] = norm_gelu(first_dot(halo[:, :16])).astype(BF16).astype(F32)
    h1[16:, :] = jnp.zeros_like(h1[16:, :])

    def first_step(step, carry):
        where = pl.ds(pl.multiple_of(step * rows, rows), rows)
        for parity, dest in ((0, e1), (1, o1)):
            acc[parity * rows : (parity + 1) * rows, :] = first_dot(patches(2 * step + parity)[:, :rows])
        for parity, dest in ((0, e1), (1, o1)):
            for r in range(0, rows, 16):
                block = acc[parity * rows + r : parity * rows + r + 16, :]
                dest[pl.ds(pl.multiple_of(step * rows + r, 16), 16), :] = norm_gelu(block).astype(BF16)
        return carry

    lax.fori_loop(0, 32, first_step, 0)

    def wrap(even, halo_ref, phases):
        rolled = pltpu.roll(even[:rows, :].astype(F32), rows - 1, 0)
        shifted = jnp.where(iota(rolled.shape, 0) == rows - 1, halo_ref[0:1, :], rolled)
        even[pl.ds(phases // 2 * rows, rows), :] = shifted.astype(BF16)

    def layer(even, odd, taps, dest_even, dest_odd, phases):
        chunk = min(phases, 4)
        size = chunk * rows

        def step(index, carry):
            base = pl.multiple_of(index * size, size)
            inputs = [even[pl.ds(base, size), :], odd[pl.ds(base, size), :]]
            if len(taps) == 3:
                inputs.append(even[pl.ds(pl.multiple_of(base + rows, rows), size), :])
            total = None
            for value, tap in zip(inputs, taps):
                term = jnp.dot(value, tap[...], preferred_element_type=F32)
                total = term if total is None else total + term
            acc[:size, :] = total
            for p in range(chunk):
                dest = dest_even if p % 2 == 0 else dest_odd
                for r in range(0, rows, 16):
                    block = acc[p * rows + r : p * rows + r + 16, :]
                    at = index * (size // 2) + p // 2 * rows + r
                    if chunk == 1:
                        at = r
                    dest[pl.ds(pl.multiple_of(at, 16), 16), :] = norm_gelu(block).astype(BF16)
            return carry

        if phases == chunk:
            step(0, 0)
        else:
            lax.fori_loop(0, phases // chunk, step, 0)

    def halo_layer(source, dest, taps):
        total = None
        for offset, tap in enumerate(taps):
            choose = jnp.where(iota((16, 24), 1) == 2.0 * iota((16, 24), 0) + offset, 1.0, 0.0)
            value = jnp.dot(
                choose.astype(BF16), source[...].astype(BF16), preferred_element_type=F32
            ).astype(BF16)
            term = jnp.dot(value, tap[...], preferred_element_type=F32)
            total = term if total is None else total + term
        dest[:8, :] = norm_gelu(total[:8]).astype(BF16).astype(F32)
        dest[8:, :] = jnp.zeros_like(dest[8:, :])

    mids = [[mid_ref.at[i, t] for t in range(3)] for i in range(4)]
    tails = [[tail_ref.at[i, t] for t in range(2)] for i in range(2)]
    ready(0)
    wrap(e1, h1, 64)
    halo_layer(h1, h2, mids[0])
    layer(e1, o1, mids[0], e2, o2, 32)
    ready(1)
    wrap(e2, h2, 32)
    halo_layer(h2, h3, mids[1])
    layer(e2, o2, mids[1], e3, o3, 16)
    ready(2)
    wrap(e3, h3, 16)
    halo_layer(h3, h1, mids[2])
    layer(e3, o3, mids[2], e4, o4, 8)
    ready(3)
    wrap(e4, h1, 8)
    layer(e4, o4, mids[3], e5, o5, 4)
    ready(4)
    layer(e5, o5, tails[0], e6, o6, 2)
    layer(e6, o6, tails[1], out_ref, out_ref, 1)


def means(n, reach, feature_ref, length_ref, out_ref, send, recv, send_sem, recv_sem):
    me = lax.axis_index("dp")
    rows, channels = feature_ref.shape
    pieces = channels // 128
    links = [(k, k - 1) for k in range(1, reach + 1)] + [(-k, reach + k - 1) for k in range(1, reach + 1)]

    def inside(k):
        return (me + k < n) & (me + k >= 0)

    base = me.astype(F32) * rows
    length_row = length_ref[...].astype(F32)
    start = starts_column(length_row)
    end = start + to_column(length_row)
    frame = iota((length_row.shape[1], rows), 1) + base
    member = (start <= frame) & (frame < end)
    start_row = jnp.sum(jnp.where(member, start, 0.0), axis=0, keepdims=True)
    end_row = jnp.sum(jnp.where(member, end, 0.0), axis=0, keepdims=True)
    start_col = to_column(start_row)
    end_col = to_column(end_row)
    features = feature_ref[...]
    line = iota((16, rows), 1) + base
    last = line >= start_row[:, rows - 1 : rows]
    initial = line < end_row[:, 0:1]
    pick = jnp.where(iota((16, rows), 0) == 0.0, jnp.where(last, 1.0, 0.0), jnp.where(initial, 1.0, 0.0))
    edges = jnp.dot(pick.astype(BF16), features, preferred_element_type=F32)
    send[...] = jnp.zeros_like(send)
    for index in range(2):
        for piece in range(pieces):
            send[index, piece : piece + 1, :] = edges[index : index + 1, piece * 128 : piece * 128 + 128]

    def copy(k, slot):
        return pltpu.make_async_remote_copy(
            src_ref=send.at[0 if k > 0 else 1],
            dst_ref=recv.at[slot],
            send_sem=send_sem.at[slot],
            recv_sem=recv_sem.at[slot],
            device_id={"dp": me + k},
        )

    for k, slot in links:
        @pl.when(inside(k))
        def _():
            copy(k, slot).start()
    local = iota((rows, rows), 1) + base
    within = jnp.where((start_col <= local) & (local < end_col), 1.0, 0.0).astype(BF16)
    totals = jnp.dot(within, features, preferred_element_type=F32)
    for k, slot in links:
        @pl.when(inside(-k))
        def _():
            copy(-k, slot).wait_recv()

        @pl.when(inside(k))
        def _():
            copy(k, slot).wait_send()
    for k, slot in links:
        row = jnp.concatenate([recv[slot, piece : piece + 1, :] for piece in range(pieces)], axis=1)
        if k > 0:
            reached = start_col <= base - (k - 1) * rows - 1.0
        else:
            reached = end_col > base - k * rows
        totals = totals + jnp.where(reached, row, 0.0)
    out_ref[...] = (features.astype(F32) - totals / (end_col - start_col)).astype(BF16)


def frontend_kernel(
    n, cap, stride, reach,
    wave_ref, slot_ref, length_ref, trim_ref, first_ref, mid_hbm, tail_hbm, out_ref,
    wide, send, recv, send_sem, recv_sem,
    mid, tail, weight_sem, features, edges, far, edge_send_sem, edge_recv_sem, *work,
):
    loads = [pltpu.make_async_copy(mid_hbm.at[i], mid.at[i], weight_sem.at[i]) for i in range(4)]
    loads.append(pltpu.make_async_copy(tail_hbm, tail, weight_sem.at[4]))
    for load in loads:
        load.start()
    far[...] = jnp.zeros_like(far)
    route(n, cap, stride, wave_ref, slot_ref, wide, send, recv, send_sem, recv_sem)
    convs(
        lambda i: loads[i].wait(),
        recv, length_ref, trim_ref, first_ref, mid, tail, features, *work,
    )
    means(n, reach, features, length_ref, out_ref, edges, far, edge_send_sem, edge_recv_sem)


def per_device(wave, row_slot, frame_lengths, sample_trim, first_weight, mid_weight, tail_weight):
    rows = wave.shape[0]
    channels = first_weight.shape[1]
    n = lax.axis_size("dp")
    cap = rows // n + 2
    stride = (cap + 1 + 7) // 8 * 8
    reach = min((MAXLEN + rows - 2) // rows, n - 1)
    vmem = pl.BlockSpec(memory_space=pltpu.VMEM)
    outside = pl.BlockSpec(memory_space=pl.ANY)

    def slab(phases):
        return pltpu.VMEM((phases * rows, channels), BF16)

    return pl.pallas_call(
        functools.partial(frontend_kernel, n, cap, stride, reach),
        out_shape=jax.ShapeDtypeStruct((rows, channels), BF16),
        in_specs=[vmem] * 5 + [outside] * 2,
        out_specs=vmem,
        scratch_shapes=[
            pltpu.VMEM((rows, WIDE), F32),
            pltpu.VMEM((n * stride, WIDE), F32),
            pltpu.VMEM((n * stride, WIDE), F32),
            pltpu.SemaphoreType.DMA((n,)),
            pltpu.SemaphoreType.DMA((n,)),
            pltpu.VMEM(mid_weight.shape, BF16),
            pltpu.VMEM(tail_weight.shape, BF16),
            pltpu.SemaphoreType.DMA((5,)),
            pltpu.VMEM((rows, channels), BF16),
            pltpu.VMEM((2, 8, 128), F32),
            pltpu.VMEM((2 * reach, 8, 128), F32),
            pltpu.SemaphoreType.DMA((2 * reach,)),
            pltpu.SemaphoreType.DMA((2 * reach,)),
            pltpu.VMEM((3, BLOCK + 16, 128), F32),
            pltpu.VMEM((16, channels), F32),
            slab(33), slab(32), slab(17), slab(16), slab(9), slab(8), slab(5), slab(4),
            slab(2), slab(2), slab(1), slab(1),
            pltpu.VMEM((24, channels), F32),
            pltpu.VMEM((24, channels), F32),
            pltpu.VMEM((24, channels), F32),
            pltpu.VMEM((4 * rows, channels), F32),
        ],
        compiler_params=pltpu.CompilerParams(
            collective_id=0, has_side_effects=True, vmem_limit_bytes=48 * 1024 * 1024
        ),
        name="frontend",
    )(
        wave, row_slot.reshape(1, -1), frame_lengths.reshape(1, -1), sample_trim.reshape(1, -1),
        first_weight, mid_weight, tail_weight,
    )


def solution(mesh):
    placed = (
        P(("groups", "dp"), None),
        P(("groups", "dp")),
        P("groups"),
        P("groups"),
        P(),
        P(),
        P(),
    )
    return jax.shard_map(
        per_device, mesh=mesh, in_specs=placed, out_specs=P(("groups", "dp"), None), check_vma=False
    )
```

```python
import functools

import jax
import jax.numpy as jnp
from jax import lax
from jax.experimental import pallas as pl
from jax.experimental.pallas import tpu as pltpu
from jax.sharding import PartitionSpec as P

BLOCK = 320
WIDE = 384
MAXLEN = 256
EPS = 1e-05
HALF_ROOT = 0.7071067811865476
HIGHEST = lax.Precision.HIGHEST
F32 = jnp.float32
BF16 = jnp.bfloat16


def iota(shape, dim):
    return lax.broadcasted_iota(jnp.int32, shape, dim).astype(F32)


def to_column(row):
    size = row.shape[1]
    same = iota((size, size), 0) == iota((size, size), 1)
    return jnp.sum(jnp.where(same, row, 0.0), axis=1, keepdims=True)


def starts_column(length_row):
    size = length_row.shape[1]
    earlier = iota((size, size), 1) < iota((size, size), 0)
    return jnp.sum(jnp.where(earlier, length_row, 0.0), axis=1, keepdims=True)


def norm_gelu(values):
    average = jnp.mean(values, axis=-1, keepdims=True)
    centred = values - average
    spread = jnp.mean(centred * centred, axis=-1, keepdims=True)
    scaled = centred * (lax.rsqrt(spread + EPS) * HALF_ROOT)
    half = scaled * HALF_ROOT
    return half + half * lax.erf(scaled)


def route(n, cap, stride, wave_ref, slot_ref, wide, send, recv, send_sem, recv_sem):
    me = lax.axis_index("dp")

    def greet(k, carry):
        pl.semaphore_signal(
            pltpu.get_barrier_semaphore(), inc=1, device_id={"dp": lax.rem(me + k, n)}
        )
        return carry

    lax.fori_loop(1, n, greet, 0)
    rows = wave_ref.shape[0]
    slot_row = slot_ref[...].astype(F32)
    slot_col = to_column(slot_row)
    target_row = jnp.floor(slot_row / rows)
    target_col = jnp.floor(slot_col / rows)
    earlier = (iota((rows, rows), 0) < iota((rows, rows), 1)) & (target_col == target_row)
    rank_row = jnp.sum(jnp.where(earlier, 1.0, 0.0), axis=0, keepdims=True)
    dest_row = target_row * stride + rank_row
    ahead_row = jnp.where(target_row * rows == slot_row, (target_row - 1.0) * stride + cap, -1.0)
    place = iota((n * stride, rows), 0)
    pick = jnp.where((place == dest_row) | (place == ahead_row), 1.0, 0.0)
    wide[:, :BLOCK] = wave_ref[...]
    wide[:, BLOCK:] = jnp.where(iota((rows, WIDE - BLOCK), 1) == 0.0, slot_col + 1.0, 0.0)
    send[...] = jnp.dot(pick, wide[...], precision=HIGHEST, preferred_element_type=F32)
    mine = pl.ds(pl.multiple_of(me * stride, stride), stride)
    recv[mine, :] = send[mine, :]
    pl.semaphore_wait(pltpu.get_barrier_semaphore(), n - 1)

    def copy_to(k):
        to = lax.rem(me + k, n)
        return pltpu.make_async_remote_copy(
            src_ref=send.at[pl.ds(pl.multiple_of(to * stride, stride), stride)],
            dst_ref=recv.at[mine],
            send_sem=send_sem.at[to],
            recv_sem=recv_sem.at[me],
            device_id={"dp": to},
        )

    def copy_from(k):
        source = lax.rem(me + n - k, n)
        return pltpu.make_async_remote_copy(
            src_ref=send.at[mine],
            dst_ref=recv.at[pl.ds(pl.multiple_of(source * stride, stride), stride)],
            send_sem=send_sem.at[me],
            recv_sem=recv_sem.at[source],
            device_id={"dp": source},
        )

    def begin(k, carry):
        copy_to(k).start()
        return carry

    def finish(k, carry):
        copy_from(k).wait_recv()
        copy_to(k).wait_send()
        return carry

    lax.fori_loop(1, n, begin, 0)
    lax.fori_loop(1, n, finish, 0)


def convs(
    ready, recv_ref, length_ref, trim_ref, first_ref, mid_ref, tail_ref, out_ref,
    xs, pad, e1, o1, e2, o2, e3, o3, e4, o4, e5, o5, e6, o6, h1, h2, h3, acc, acc2,
):
    me = lax.axis_index("dp").astype(F32)
    rows = out_ref.shape[0]
    length_row = length_ref[...].astype(F32)
    trim_col = to_column(trim_ref[...].astype(F32))
    start = starts_column(length_row)
    end = start + to_column(length_row)
    count = length_row.shape[1]
    frame = iota((count, 128), 1) + me * rows
    limit = jnp.sum(
        jnp.where((start <= frame) & (frame < end), BLOCK * (end - frame) - trim_col, 0.0),
        axis=0,
        keepdims=True,
    )
    got = recv_ref.shape[0]
    slot = recv_ref[:, BLOCK : BLOCK + 1] - 1.0 - me * rows
    lane = iota((got, 128), 1)
    spread = jnp.where((slot == lane) & (lane <= rows), 1.0, 0.0)
    wave = jnp.transpose(recv_ref[...])[:BLOCK]
    stream = jnp.dot(wave, spread, precision=HIGHEST, preferred_element_type=F32)
    signal = jnp.where(iota((BLOCK, 128), 0) < limit, stream, 0.0)
    part1 = signal.astype(BF16).astype(F32)
    rest = signal - part1
    part2 = rest.astype(BF16).astype(F32)
    part3 = rest - part2
    for index, part in enumerate((part1, part2, part3)):
        xs[index, :BLOCK, :] = part
        xs[index, BLOCK : BLOCK + 8, :] = pltpu.roll(part[:8], 127, 1)
        xs[index, BLOCK + 8 :, :] = jnp.zeros((8, 128), F32)

    pad[...] = jnp.zeros_like(pad)
    pad[: first_ref.shape[0], :] = first_ref[...]
    first = pad[...]
    weight1 = first.astype(BF16).astype(F32)
    left = first - weight1
    weight2 = left.astype(BF16).astype(F32)
    weight3 = left - weight2
    kernel1 = jnp.concatenate([weight1, weight2, weight1, weight2, weight3, weight1], axis=0).astype(BF16)

    def patches(phase):
        a, b, c = [xs[index, pl.ds(5 * phase, 16), :] for index in range(3)]
        return jnp.concatenate([a, a, b, b, a, c], axis=0)

    def first_dot(block):
        return lax.dot_general(
            block.astype(BF16), kernel1, (((0,), (0,)), ((), ())), preferred_element_type=F32
        )

    def gather_halo(phase, total):
        return jnp.where(
            lax.broadcasted_iota(jnp.int32, (96, 128), 1) == phase, patches(phase)[:, rows : rows + 1], total
        )

    halo = lax.fori_loop(0, 16, gather_halo, jnp.zeros((96, 128), F32))
    h1[:16, :] = norm_gelu(first_dot(halo[:, :16])).astype(BF16).astype(F32)
    h1[16:, :] = jnp.zeros_like(h1[16:, :])

    def pipeline(count, multiply, finish):
        multiply(0, acc)
        if count == 1:
            finish(0, acc)
            return

        def pair(j, carry):
            multiply(2 * j + 1, acc2)
            finish(2 * j, acc)
            multiply(2 * j + 2, acc)
            finish(2 * j + 1, acc2)
            return carry

        if count > 2:
            lax.fori_loop(0, count // 2 - 1, pair, 0)
        multiply(count - 1, acc2)
        finish(count - 2, acc)
        finish(count - 1, acc2)

    left_half = lax.broadcasted_iota(jnp.int32, (16, 128), 1) < rows

    def first_multiply(step, into):
        joined = []
        for index in range(3):
            even = xs[index, pl.ds(10 * step, 16), :]
            odd = xs[index, pl.ds(10 * step + 5, 16), :]
            joined.append(jnp.where(left_half, even, pltpu.roll(odd, rows, 1)))
        a, b, c = joined
        into[: 2 * rows, :] = first_dot(jnp.concatenate([a, a, b, b, a, c], axis=0))

    def first_finish(step, source):
        for parity, dest in ((0, e1), (1, o1)):
            for r in range(0, rows, 16):
                block = source[parity * rows + r : parity * rows + r + 16, :]
                dest[pl.ds(pl.multiple_of(step * rows + r, 16), 16), :] = norm_gelu(block).astype(BF16)

    pipeline(32, first_multiply, first_finish)

    def wrap(even, halo_ref, phases):
        rolled = pltpu.roll(even[:rows, :].astype(F32), rows - 1, 0)
        shifted = jnp.where(iota(rolled.shape, 0) == rows - 1, halo_ref[0:1, :], rolled)
        even[pl.ds(phases // 2 * rows, rows), :] = shifted.astype(BF16)

    def layer(even, odd, weight, count, dest_even, dest_odd, phases):
        chunk = min(phases, 4)
        size = chunk * rows

        def multiply(index, into):
            base = index * size
            inputs = [even[pl.ds(base, size), :], odd[pl.ds(base, size), :]]
            if count == 3:
                inputs.append(even[pl.ds(base + rows, size), :])
            into[:size, :] = jnp.dot(
                jnp.concatenate(inputs, axis=1), weight[...], preferred_element_type=F32
            )

        def finish(index, source):
            for p in range(chunk):
                dest = dest_even if p % 2 == 0 else dest_odd
                for r in range(0, rows, 16):
                    block = source[p * rows + r : p * rows + r + 16, :]
                    at = index * (size // 2) + p // 2 * rows + r
                    dest[pl.ds(at, 16), :] = norm_gelu(block).astype(BF16)

        pipeline(phases // chunk, multiply, finish)

    def halo_layer(source, dest, weight):
        taps = []
        for offset in range(3):
            choose = jnp.where(iota((16, 24), 1) == 2.0 * iota((16, 24), 0) + offset, 1.0, 0.0)
            taps.append(
                jnp.dot(
                    choose.astype(BF16), source[...].astype(BF16), preferred_element_type=F32
                ).astype(BF16)
            )
        total = jnp.dot(jnp.concatenate(taps, axis=1), weight[...], preferred_element_type=F32)
        dest[:8, :] = norm_gelu(total[:8]).astype(BF16).astype(F32)
        dest[8:, :] = jnp.zeros_like(dest[8:, :])

    mids = [mid_ref.at[i] for i in range(4)]
    tails = [tail_ref.at[i] for i in range(2)]
    ready(0)
    wrap(e1, h1, 64)
    halo_layer(h1, h2, mids[0])
    layer(e1, o1, mids[0], 3, e2, o2, 32)
    ready(1)
    wrap(e2, h2, 32)
    halo_layer(h2, h3, mids[1])
    layer(e2, o2, mids[1], 3, e3, o3, 16)
    ready(2)
    wrap(e3, h3, 16)
    halo_layer(h3, h1, mids[2])
    layer(e3, o3, mids[2], 3, e4, o4, 8)
    ready(3)
    wrap(e4, h1, 8)
    layer(e4, o4, mids[3], 3, e5, o5, 4)
    ready(4)
    layer(e5, o5, tails[0], 2, e6, o6, 2)
    layer(e6, o6, tails[1], 2, out_ref, out_ref, 1)


def means(n, reach, feature_ref, length_ref, out_ref, send, recv, send_sem, recv_sem):
    me = lax.axis_index("dp")
    rows, channels = feature_ref.shape
    pieces = channels // 128
    links = [(k, k - 1) for k in range(1, reach + 1)] + [(-k, reach + k - 1) for k in range(1, reach + 1)]

    def inside(k):
        return (me + k < n) & (me + k >= 0)

    base = me.astype(F32) * rows
    length_row = length_ref[...].astype(F32)
    start = starts_column(length_row)
    end = start + to_column(length_row)
    frame = iota((length_row.shape[1], rows), 1) + base
    member = (start <= frame) & (frame < end)
    start_row = jnp.sum(jnp.where(member, start, 0.0), axis=0, keepdims=True)
    end_row = jnp.sum(jnp.where(member, end, 0.0), axis=0, keepdims=True)
    start_col = to_column(start_row)
    end_col = to_column(end_row)
    features = feature_ref[...]
    line = iota((16, rows), 1) + base
    last = line >= start_row[:, rows - 1 : rows]
    initial = line < end_row[:, 0:1]
    pick = jnp.where(iota((16, rows), 0) == 0.0, jnp.where(last, 1.0, 0.0), jnp.where(initial, 1.0, 0.0))
    edges = jnp.dot(pick.astype(BF16), features, preferred_element_type=F32)
    send[...] = jnp.zeros_like(send)
    for index in range(2):
        for piece in range(pieces):
            send[index, piece : piece + 1, :] = edges[index : index + 1, piece * 128 : piece * 128 + 128]

    def copy(k, slot):
        return pltpu.make_async_remote_copy(
            src_ref=send.at[0 if k > 0 else 1],
            dst_ref=recv.at[slot],
            send_sem=send_sem.at[slot],
            recv_sem=recv_sem.at[slot],
            device_id={"dp": me + k},
        )

    for k, slot in links:
        @pl.when(inside(k))
        def _():
            copy(k, slot).start()
    local = iota((rows, rows), 1) + base
    within = jnp.where((start_col <= local) & (local < end_col), 1.0, 0.0).astype(BF16)
    totals = jnp.dot(within, features, preferred_element_type=F32)
    for k, slot in links:
        @pl.when(inside(-k))
        def _():
            copy(-k, slot).wait_recv()

        @pl.when(inside(k))
        def _():
            copy(k, slot).wait_send()
    for k, slot in links:
        row = jnp.concatenate([recv[slot, piece : piece + 1, :] for piece in range(pieces)], axis=1)
        if k > 0:
            reached = start_col <= base - (k - 1) * rows - 1.0
        else:
            reached = end_col > base - k * rows
        totals = totals + jnp.where(reached, row, 0.0)
    out_ref[...] = (features.astype(F32) - totals / (end_col - start_col)).astype(BF16)


def frontend_kernel(
    n, cap, stride, reach,
    wave_ref, slot_ref, length_ref, trim_ref, first_ref, mid_hbm, tail_hbm, out_ref,
    wide, send, recv, send_sem, recv_sem,
    mid, tail, weight_sem, features, edges, far, edge_send_sem, edge_recv_sem, *work,
):
    loads = [pltpu.make_async_copy(mid_hbm.at[i], mid.at[i], weight_sem.at[i]) for i in range(4)]
    loads.append(pltpu.make_async_copy(tail_hbm, tail, weight_sem.at[4]))
    for load in loads:
        load.start()
    far[...] = jnp.zeros_like(far)
    route(n, cap, stride, wave_ref, slot_ref, wide, send, recv, send_sem, recv_sem)
    convs(
        lambda i: loads[i].wait(),
        recv, length_ref, trim_ref, first_ref, mid, tail, features, *work,
    )
    means(n, reach, features, length_ref, out_ref, edges, far, edge_send_sem, edge_recv_sem)


def per_device(wave, row_slot, frame_lengths, sample_trim, first_weight, mid_weight, tail_weight):
    rows = wave.shape[0]
    channels = first_weight.shape[1]
    n = lax.axis_size("dp")
    cap = rows // n + 2
    stride = (cap + 1 + 7) // 8 * 8
    reach = min((MAXLEN + rows - 2) // rows, n - 1)
    mid = mid_weight.reshape(4, 3 * channels, channels)
    tail = tail_weight.reshape(2, 2 * channels, channels)
    vmem = pl.BlockSpec(memory_space=pltpu.VMEM)
    outside = pl.BlockSpec(memory_space=pl.ANY)

    def slab(phases):
        return pltpu.VMEM((phases * rows, channels), BF16)

    return pl.pallas_call(
        functools.partial(frontend_kernel, n, cap, stride, reach),
        out_shape=jax.ShapeDtypeStruct((rows, channels), BF16),
        in_specs=[vmem] * 5 + [outside] * 2,
        out_specs=vmem,
        scratch_shapes=[
            pltpu.VMEM((rows, WIDE), F32),
            pltpu.VMEM((n * stride, WIDE), F32),
            pltpu.VMEM((n * stride, WIDE), F32),
            pltpu.SemaphoreType.DMA((n,)),
            pltpu.SemaphoreType.DMA((n,)),
            pltpu.VMEM(mid.shape, BF16),
            pltpu.VMEM(tail.shape, BF16),
            pltpu.SemaphoreType.DMA((5,)),
            pltpu.VMEM((rows, channels), BF16),
            pltpu.VMEM((2, 8, 128), F32),
            pltpu.VMEM((2 * reach, 8, 128), F32),
            pltpu.SemaphoreType.DMA((2 * reach,)),
            pltpu.SemaphoreType.DMA((2 * reach,)),
            pltpu.VMEM((3, BLOCK + 16, 128), F32),
            pltpu.VMEM((16, channels), F32),
            slab(33), slab(32), slab(17), slab(16), slab(9), slab(8), slab(5), slab(4),
            slab(2), slab(2), slab(1), slab(1),
            pltpu.VMEM((24, channels), F32),
            pltpu.VMEM((24, channels), F32),
            pltpu.VMEM((24, channels), F32),
            pltpu.VMEM((4 * rows, channels), F32),
            pltpu.VMEM((4 * rows, channels), F32),
        ],
        compiler_params=pltpu.CompilerParams(
            collective_id=0, has_side_effects=True, vmem_limit_bytes=48 * 1024 * 1024
        ),
        name="frontend",
    )(
        wave, row_slot.reshape(1, -1), frame_lengths.reshape(1, -1), sample_trim.reshape(1, -1),
        first_weight, mid, tail,
    )


def solution(mesh):
    placed = (
        P(("groups", "dp"), None),
        P(("groups", "dp")),
        P("groups"),
        P("groups"),
        P(),
        P(),
        P(),
    )
    return jax.shard_map(
        per_device, mesh=mesh, in_specs=placed, out_specs=P(("groups", "dp"), None), check_vma=False
    )
```

```python
import functools

import jax
import jax.numpy as jnp
from jax import lax
from jax.experimental import pallas as pl
from jax.experimental.pallas import tpu as pltpu
from jax.sharding import PartitionSpec as P

BLOCK = 320
WIDE = 384
MAXLEN = 256
EPS = 1e-05
HALF_ROOT = 0.7071067811865476
HIGHEST = lax.Precision.HIGHEST
F32 = jnp.float32
BF16 = jnp.bfloat16


def iota(shape, dim):
    return lax.broadcasted_iota(jnp.int32, shape, dim).astype(F32)


def to_column(row):
    size = row.shape[1]
    same = iota((size, size), 0) == iota((size, size), 1)
    return jnp.sum(jnp.where(same, row, 0.0), axis=1, keepdims=True)


def starts_column(length_row):
    size = length_row.shape[1]
    earlier = iota((size, size), 1) < iota((size, size), 0)
    return jnp.sum(jnp.where(earlier, length_row, 0.0), axis=1, keepdims=True)


def norm_gelu(values):
    average = jnp.mean(values, axis=-1, keepdims=True)
    return scale_gelu(values - average)


def scale_gelu(centred):
    spread = jnp.mean(centred * centred, axis=-1, keepdims=True)
    scaled = centred * (lax.rsqrt(spread + EPS) * HALF_ROOT)
    half = scaled * HALF_ROOT
    return half + half * lax.erf(scaled)


def route(n, cap, stride, wave_ref, slot_ref, wide, send, recv, send_sem, recv_sem):
    me = lax.axis_index("dp")

    def greet(k, carry):
        pl.semaphore_signal(
            pltpu.get_barrier_semaphore(), inc=1, device_id={"dp": lax.rem(me + k, n)}
        )
        return carry

    lax.fori_loop(1, n, greet, 0)
    rows = wave_ref.shape[0]
    slot_row = slot_ref[...].astype(F32)
    slot_col = to_column(slot_row)
    target_row = jnp.floor(slot_row / rows)
    target_col = jnp.floor(slot_col / rows)
    earlier = (iota((rows, rows), 0) < iota((rows, rows), 1)) & (target_col == target_row)
    rank_row = jnp.sum(jnp.where(earlier, 1.0, 0.0), axis=0, keepdims=True)
    dest_row = target_row * stride + rank_row
    ahead_row = jnp.where(target_row * rows == slot_row, (target_row - 1.0) * stride + cap, -1.0)
    place = iota((n * stride, rows), 0)
    pick = jnp.where((place == dest_row) | (place == ahead_row), 1.0, 0.0)
    wide[:, :BLOCK] = wave_ref[...]
    wide[:, BLOCK:] = jnp.where(iota((rows, WIDE - BLOCK), 1) == 0.0, slot_col + 1.0, 0.0)
    send[...] = jnp.dot(pick, wide[...], precision=HIGHEST, preferred_element_type=F32)
    mine = pl.ds(pl.multiple_of(me * stride, stride), stride)
    recv[mine, :] = send[mine, :]
    pl.semaphore_wait(pltpu.get_barrier_semaphore(), n - 1)

    def copy_to(k):
        to = lax.rem(me + k, n)
        return pltpu.make_async_remote_copy(
            src_ref=send.at[pl.ds(pl.multiple_of(to * stride, stride), stride)],
            dst_ref=recv.at[mine],
            send_sem=send_sem.at[to],
            recv_sem=recv_sem.at[me],
            device_id={"dp": to},
        )

    def copy_from(k):
        source = lax.rem(me + n - k, n)
        return pltpu.make_async_remote_copy(
            src_ref=send.at[mine],
            dst_ref=recv.at[pl.ds(pl.multiple_of(source * stride, stride), stride)],
            send_sem=send_sem.at[me],
            recv_sem=recv_sem.at[source],
            device_id={"dp": source},
        )

    def begin(k, carry):
        copy_to(k).start()
        return carry

    def finish(k, carry):
        copy_from(k).wait_recv()
        copy_to(k).wait_send()
        return carry

    lax.fori_loop(1, n, begin, 0)
    lax.fori_loop(1, n, finish, 0)


def convs(
    ready, recv_ref, length_ref, trim_ref, first_ref, mid_ref, tail_ref, out_ref,
    xs, pad, e1, o1, e2, o2, e3, o3, e4, o4, e5, o5, e6, o6, h1, h2, h3, acc, acc2,
):
    me = lax.axis_index("dp").astype(F32)
    rows = out_ref.shape[0]
    length_row = length_ref[...].astype(F32)
    trim_col = to_column(trim_ref[...].astype(F32))
    start = starts_column(length_row)
    end = start + to_column(length_row)
    count = length_row.shape[1]
    frame = iota((count, 128), 1) + me * rows
    limit = jnp.sum(
        jnp.where((start <= frame) & (frame < end), BLOCK * (end - frame) - trim_col, 0.0),
        axis=0,
        keepdims=True,
    )
    got = recv_ref.shape[0]
    slot = recv_ref[:, BLOCK : BLOCK + 1] - 1.0 - me * rows
    lane = iota((got, 128), 1)
    spread = jnp.where((slot == lane) & (lane <= rows), 1.0, 0.0)
    wave = jnp.transpose(recv_ref[...])[:BLOCK]
    stream = jnp.dot(wave, spread, precision=HIGHEST, preferred_element_type=F32)
    signal = jnp.where(iota((BLOCK, 128), 0) < limit, stream, 0.0)
    part1 = signal.astype(BF16).astype(F32)
    rest = signal - part1
    part2 = rest.astype(BF16).astype(F32)
    part3 = rest - part2
    for index, part in enumerate((part1, part2, part3)):
        xs[index, :BLOCK, :] = part
        xs[index, BLOCK : BLOCK + 8, :] = pltpu.roll(part[:8], 127, 1)
        xs[index, BLOCK + 8 :, :] = jnp.zeros((8, 128), F32)

    pad[...] = jnp.zeros_like(pad)
    pad[: first_ref.shape[0], :] = first_ref[...]
    first = pad[...] - jnp.mean(pad[...], axis=-1, keepdims=True)
    weight1 = first.astype(BF16).astype(F32)
    left = first - weight1
    weight2 = left.astype(BF16).astype(F32)
    weight3 = left - weight2
    kernel1 = jnp.concatenate([weight1, weight2, weight1, weight2, weight3, weight1], axis=0).astype(BF16)

    def patches(phase):
        a, b, c = [xs[index, pl.ds(5 * phase, 16), :] for index in range(3)]
        return jnp.concatenate([a, a, b, b, a, c], axis=0)

    def first_dot(block):
        return lax.dot_general(
            block.astype(BF16), kernel1, (((0,), (0,)), ((), ())), preferred_element_type=F32
        )

    def gather_halo(phase, total):
        return jnp.where(
            lax.broadcasted_iota(jnp.int32, (96, 128), 1) == phase, patches(phase)[:, rows : rows + 1], total
        )

    halo = lax.fori_loop(0, 16, gather_halo, jnp.zeros((96, 128), F32))
    h1[:16, :] = scale_gelu(first_dot(halo[:, :16])).astype(BF16).astype(F32)
    h1[16:, :] = jnp.zeros_like(h1[16:, :])

    def pipeline(count, multiply, finish):
        multiply(0, acc)
        if count == 1:
            finish(0, acc)
            return

        def pair(j, carry):
            multiply(2 * j + 1, acc2)
            finish(2 * j, acc)
            multiply(2 * j + 2, acc)
            finish(2 * j + 1, acc2)
            return carry

        if count > 2:
            lax.fori_loop(0, count // 2 - 1, pair, 0)
        multiply(count - 1, acc2)
        finish(count - 2, acc)
        finish(count - 1, acc2)

    left_half = lax.broadcasted_iota(jnp.int32, (16, 128), 1) < rows

    def first_multiply(step, into):
        joined = []
        for index in range(3):
            even = xs[index, pl.ds(10 * step, 16), :]
            odd = xs[index, pl.ds(10 * step + 5, 16), :]
            joined.append(jnp.where(left_half, even, pltpu.roll(odd, rows, 1)))
        a, b, c = joined
        into[: 2 * rows, :] = first_dot(jnp.concatenate([a, a, b, b, a, c], axis=0))

    def first_finish(step, source):
        for parity, dest in ((0, e1), (1, o1)):
            for r in range(0, rows, 16):
                block = source[parity * rows + r : parity * rows + r + 16, :]
                dest[pl.ds(pl.multiple_of(step * rows + r, 16), 16), :] = scale_gelu(block).astype(BF16)

    pipeline(32, first_multiply, first_finish)

    def wrap(even, halo_ref, phases):
        rolled = pltpu.roll(even[:rows, :].astype(F32), rows - 1, 0)
        shifted = jnp.where(iota(rolled.shape, 0) == rows - 1, halo_ref[0:1, :], rolled)
        even[pl.ds(phases // 2 * rows, rows), :] = shifted.astype(BF16)

    def layer(even, odd, weight, count, dest_even, dest_odd, phases):
        chunk = min(phases, 4)
        size = chunk * rows

        def multiply(index, into):
            base = index * size
            inputs = [even[pl.ds(base, size), :], odd[pl.ds(base, size), :]]
            if count == 3:
                inputs.append(even[pl.ds(base + rows, size), :])
            into[:size, :] = jnp.dot(
                jnp.concatenate(inputs, axis=1), weight[...], preferred_element_type=F32
            )

        def finish(index, source):
            for p in range(chunk):
                dest = dest_even if p % 2 == 0 else dest_odd
                for r in range(0, rows, 16):
                    block = source[p * rows + r : p * rows + r + 16, :]
                    at = index * (size // 2) + p // 2 * rows + r
                    dest[pl.ds(at, 16), :] = norm_gelu(block).astype(BF16)

        pipeline(phases // chunk, multiply, finish)

    def halo_layer(source, dest, weight):
        taps = []
        for offset in range(3):
            choose = jnp.where(iota((16, 24), 1) == 2.0 * iota((16, 24), 0) + offset, 1.0, 0.0)
            taps.append(
                jnp.dot(
                    choose.astype(BF16), source[...].astype(BF16), preferred_element_type=F32
                ).astype(BF16)
            )
        total = jnp.dot(jnp.concatenate(taps, axis=1), weight[...], preferred_element_type=F32)
        dest[:8, :] = norm_gelu(total[:8]).astype(BF16).astype(F32)
        dest[8:, :] = jnp.zeros_like(dest[8:, :])

    mids = [mid_ref.at[i] for i in range(4)]
    tails = [tail_ref.at[i] for i in range(2)]
    ready(0)
    wrap(e1, h1, 64)
    halo_layer(h1, h2, mids[0])
    layer(e1, o1, mids[0], 3, e2, o2, 32)
    ready(1)
    wrap(e2, h2, 32)
    halo_layer(h2, h3, mids[1])
    layer(e2, o2, mids[1], 3, e3, o3, 16)
    ready(2)
    wrap(e3, h3, 16)
    halo_layer(h3, h1, mids[2])
    layer(e3, o3, mids[2], 3, e4, o4, 8)
    ready(3)
    wrap(e4, h1, 8)
    layer(e4, o4, mids[3], 3, e5, o5, 4)
    ready(4)
    layer(e5, o5, tails[0], 2, e6, o6, 2)
    layer(e6, o6, tails[1], 2, out_ref, out_ref, 1)


def means(n, reach, feature_ref, length_ref, out_ref, send, recv, send_sem, recv_sem):
    me = lax.axis_index("dp")
    rows, channels = feature_ref.shape
    pieces = channels // 128
    links = [(k, k - 1) for k in range(1, reach + 1)] + [(-k, reach + k - 1) for k in range(1, reach + 1)]

    def inside(k):
        return (me + k < n) & (me + k >= 0)

    base = me.astype(F32) * rows
    length_row = length_ref[...].astype(F32)
    start = starts_column(length_row)
    end = start + to_column(length_row)
    frame = iota((length_row.shape[1], rows), 1) + base
    member = (start <= frame) & (frame < end)
    start_row = jnp.sum(jnp.where(member, start, 0.0), axis=0, keepdims=True)
    end_row = jnp.sum(jnp.where(member, end, 0.0), axis=0, keepdims=True)
    start_col = to_column(start_row)
    end_col = to_column(end_row)
    features = feature_ref[...]
    line = iota((16, rows), 1) + base
    last = line >= start_row[:, rows - 1 : rows]
    initial = line < end_row[:, 0:1]
    pick = jnp.where(iota((16, rows), 0) == 0.0, jnp.where(last, 1.0, 0.0), jnp.where(initial, 1.0, 0.0))
    edges = jnp.dot(pick.astype(BF16), features, preferred_element_type=F32)
    send[...] = jnp.zeros_like(send)
    for index in range(2):
        for piece in range(pieces):
            send[index, piece : piece + 1, :] = edges[index : index + 1, piece * 128 : piece * 128 + 128]

    def copy(k, slot):
        return pltpu.make_async_remote_copy(
            src_ref=send.at[0 if k > 0 else 1],
            dst_ref=recv.at[slot],
            send_sem=send_sem.at[slot],
            recv_sem=recv_sem.at[slot],
            device_id={"dp": me + k},
        )

    for k, slot in links:
        @pl.when(inside(k))
        def _():
            copy(k, slot).start()
    local = iota((rows, rows), 1) + base
    within = jnp.where((start_col <= local) & (local < end_col), 1.0, 0.0).astype(BF16)
    totals = jnp.dot(within, features, preferred_element_type=F32)
    for k, slot in links:
        @pl.when(inside(-k))
        def _():
            copy(-k, slot).wait_recv()

        @pl.when(inside(k))
        def _():
            copy(k, slot).wait_send()
    for k, slot in links:
        row = jnp.concatenate([recv[slot, piece : piece + 1, :] for piece in range(pieces)], axis=1)
        if k > 0:
            reached = start_col <= base - (k - 1) * rows - 1.0
        else:
            reached = end_col > base - k * rows
        totals = totals + jnp.where(reached, row, 0.0)
    out_ref[...] = (features.astype(F32) - totals / (end_col - start_col)).astype(BF16)


def frontend_kernel(
    n, cap, stride, reach,
    wave_ref, slot_ref, length_ref, trim_ref, first_ref, mid_hbm, tail_hbm, out_ref,
    wide, send, recv, send_sem, recv_sem,
    mid, tail, weight_sem, features, edges, far, edge_send_sem, edge_recv_sem, *work,
):
    loads = [pltpu.make_async_copy(mid_hbm.at[i], mid.at[i], weight_sem.at[i]) for i in range(4)]
    loads.append(pltpu.make_async_copy(tail_hbm, tail, weight_sem.at[4]))
    for load in loads:
        load.start()
    far[...] = jnp.zeros_like(far)
    route(n, cap, stride, wave_ref, slot_ref, wide, send, recv, send_sem, recv_sem)
    convs(
        lambda i: loads[i].wait(),
        recv, length_ref, trim_ref, first_ref, mid, tail, features, *work,
    )
    means(n, reach, features, length_ref, out_ref, edges, far, edge_send_sem, edge_recv_sem)


def per_device(wave, row_slot, frame_lengths, sample_trim, first_weight, mid_weight, tail_weight):
    rows = wave.shape[0]
    channels = first_weight.shape[1]
    n = lax.axis_size("dp")
    cap = rows // n + 2
    stride = (cap + 1 + 7) // 8 * 8
    reach = min((MAXLEN + rows - 2) // rows, n - 1)
    mid = mid_weight.reshape(4, 3 * channels, channels)
    tail = tail_weight.reshape(2, 2 * channels, channels)
    vmem = pl.BlockSpec(memory_space=pltpu.VMEM)
    outside = pl.BlockSpec(memory_space=pl.ANY)

    def slab(phases):
        return pltpu.VMEM((phases * rows, channels), BF16)

    return pl.pallas_call(
        functools.partial(frontend_kernel, n, cap, stride, reach),
        out_shape=jax.ShapeDtypeStruct((rows, channels), BF16),
        in_specs=[vmem] * 5 + [outside] * 2,
        out_specs=vmem,
        scratch_shapes=[
            pltpu.VMEM((rows, WIDE), F32),
            pltpu.VMEM((n * stride, WIDE), F32),
            pltpu.VMEM((n * stride, WIDE), F32),
            pltpu.SemaphoreType.DMA((n,)),
            pltpu.SemaphoreType.DMA((n,)),
            pltpu.VMEM(mid.shape, BF16),
            pltpu.VMEM(tail.shape, BF16),
            pltpu.SemaphoreType.DMA((5,)),
            pltpu.VMEM((rows, channels), BF16),
            pltpu.VMEM((2, 8, 128), F32),
            pltpu.VMEM((2 * reach, 8, 128), F32),
            pltpu.SemaphoreType.DMA((2 * reach,)),
            pltpu.SemaphoreType.DMA((2 * reach,)),
            pltpu.VMEM((3, BLOCK + 16, 128), F32),
            pltpu.VMEM((16, channels), F32),
            slab(33), slab(32), slab(17), slab(16), slab(9), slab(8), slab(5), slab(4),
            slab(2), slab(2), slab(1), slab(1),
            pltpu.VMEM((24, channels), F32),
            pltpu.VMEM((24, channels), F32),
            pltpu.VMEM((24, channels), F32),
            pltpu.VMEM((4 * rows, channels), F32),
            pltpu.VMEM((4 * rows, channels), F32),
        ],
        compiler_params=pltpu.CompilerParams(
            collective_id=0, has_side_effects=True, vmem_limit_bytes=48 * 1024 * 1024
        ),
        name="frontend",
    )(
        wave, row_slot.reshape(1, -1), frame_lengths.reshape(1, -1), sample_trim.reshape(1, -1),
        first_weight, mid, tail,
    )


def solution(mesh):
    placed = (
        P(("groups", "dp"), None),
        P(("groups", "dp")),
        P("groups"),
        P("groups"),
        P(),
        P(),
        P(),
    )
    return jax.shard_map(
        per_device, mesh=mesh, in_specs=placed, out_specs=P(("groups", "dp"), None), check_vma=False
    )
```
